32 devices in a mesh: src: 16 (over z, x, core), tgt: 2 (over y).
Axes of the slice: x: 2, y: 2, z: 4, core: 2. Of those that a mesh axis runs over, the one named last changes fastest.
Arguments:
- source_embed: bfloat16 [128, 65536], P(None, 'src'), may hold values from -1 to 1
- target_embed: bfloat16 [128, 1024], P(None, 'tgt'), may hold values from -1 to 1
- source_expr: bfloat16 [128, 65536], P(None, 'src'), may hold values from -0.5390625 to 0.5390625
- target_expr: bfloat16 [128, 1024], P(None, 'tgt'), may hold values from -0.5390625 to 0.5390625
- current_plan: bfloat16 [65536, 1024], P('src', 'tgt'), as said below
- source_mass: float32 [65536], P('src'), may hold values from 0.25 to 4
- target_mass: float32 [1024], P('tgt'), may hold values from 0.25 to 4
- source_potential: float32 [65536], P('src'), may hold values from -16 to 16
- target_genes: bfloat16 [1024, 256], P('tgt'), may hold values from -6 to 6
Outputs:
- imputed: bfloat16 [65536, 256], P(('src', 'tgt'))
The draws below stay inside these ranges and needn't reach their ends.
Inputs may be any that keep to these rules, and one draw needn't show every extreme that they name: Every entry of current_plan is positive.
All inputs are finite; a program needn't handle non-finite values.
Results may differ from the reference program's by a relative error of at most 0.014.
Values may be sent and summed in bfloat16 or wider, within the bound.
A program may use at most 64 MiB of HBM per device.

```python
import math
import jax
import jax.numpy as jnp
from jax import lax

D = 128
GENES = 256
ITERS = 2
RANK = 130
NS = 65536
NT = 1024


group_count = 256


def cluster_labels(key, amount, salt_value):
    return jax.random.randint(jax.random.fold_in(key, salt_value), (amount,), 0, group_count)


def embed_spots(key, labels, salt_value):
    centres = jax.random.normal(jax.random.fold_in(key, 101), (D, group_count), jnp.float32) * 0.075
    placed = jnp.take(centres, labels, axis=1)
    amount = labels.shape[0]
    values = placed + 0.05 * jax.random.normal(jax.random.fold_in(key, salt_value), (D, amount), jnp.float32)
    return jnp.clip(values, -1.0, 1.0).astype(jnp.bfloat16)


def draw_source_embed(key, part):
    return embed_spots(key, cluster_labels(key, NS, 202), 11)


def draw_target_embed(key, part):
    return embed_spots(key, cluster_labels(key, NT, 303), 21)


def draw_current_plan(key, part):
    label_src = cluster_labels(key, NS, 202)
    label_tgt = cluster_labels(key, NT, 303)
    matched = (label_src[:, None] == label_tgt[None, :]).astype(jnp.float32)
    rising = 0.5 + (jnp.arange(NS, dtype=jnp.float32) + 0.5) / NS
    jitter = jnp.exp(0.5 * jnp.clip(jax.random.normal(jax.random.fold_in(key, 404), (NS, NT), jnp.float32), -6.0, 6.0))
    entries = jitter * (1.0 + 1024.0 * matched) * rising[:, None] / 5.67
    return entries.astype(jnp.bfloat16)


def draw_source_potential(key, part):
    base = 0.1 * jnp.clip(jax.random.normal(jax.random.fold_in(key, 505), (NS,), jnp.float32), -4.0, 4.0)
    group_level = jnp.exp(jax.random.uniform(jax.random.fold_in(key, 606), (NS // 32,), jnp.float32, math.log(4.0), math.log(14.0)))
    tie_gap = jax.random.uniform(jax.random.fold_in(key, 707), (NS // 32,), jnp.float32, 0.05, 0.15)
    position = jnp.arange(NS, dtype=jnp.int32) % 32
    level = jnp.repeat(group_level, 32)
    gap = jnp.repeat(tie_gap, 32)
    first = (position == 3).astype(jnp.float32)
    second = (position == 4).astype(jnp.float32)
    bumped = first * level + second * (level + gap)
    return base * (1.0 - first - second) + bumped


def block_scale(key, shape, shards, smallest, top_value):
    def one(axis_at, blocks):
        steps = jax.random.uniform(jax.random.fold_in(jax.random.fold_in(key, 6), axis_at), (blocks,), jnp.float32, smallest / len(shards), top_value / len(shards))
        return jnp.repeat(jnp.exp(steps), shape[axis_at] // blocks).reshape((-1,) + (1,) * (len(shape) - axis_at - 1))

    gain = one(*shards[0])
    for cut in shards[1:]:
        gain = gain * one(*cut)
    return gain


def bell_draw(stream_key, shape, width, bound, split=(), held_as=jnp.bfloat16):
    values = jax.random.normal(stream_key, shape, jnp.float32) * width
    if len(split) > 0:
        values = block_scale(stream_key, shape, split, -0.22, 0.18) * values
    return jnp.clip(values, min=-bound, max=bound).astype(held_as)


def setup_inputs(seed: int = 0) -> dict:
    keys = jax.random.split(jax.random.key(seed), 10)
    source_embed = draw_source_embed(jax.random.fold_in(keys[9], 71), 0)
    target_embed = draw_target_embed(jax.random.fold_in(keys[9], 71), 0)
    source_expr = bell_draw(keys[2], (D, NS), 0.09, 0.5390625, ((1, 16),))
    target_expr = bell_draw(keys[3], (D, NT), 0.09, 0.5390625, ((1, 2),))
    current_plan = draw_current_plan(jax.random.fold_in(keys[9], 71), 0)
    source_mass = jnp.clip(jnp.exp(math.log(4.0) - 2.7725887 * jax.random.uniform(keys[5], (NS,), jnp.float32) ** block_scale(keys[5], (NS,), ((0, 16),), -0.2, 0.2)), 0.25, 4.0)
    target_mass = jnp.clip(jnp.exp(math.log(4.0) - 2.7725887 * jax.random.uniform(keys[6], (NT,), jnp.float32) ** block_scale(keys[6], (NT,), ((0, 2),), -0.2, 0.2)), 0.25, 4.0)
    source_potential = draw_source_potential(jax.random.fold_in(keys[9], 71), 0)
    target_genes = bell_draw(keys[8], (NT, GENES), 1.0, 6.0, ((0, 2),))
    return dict(source_embed=source_embed, target_embed=target_embed, source_expr=source_expr, target_expr=target_expr, current_plan=current_plan, source_mass=source_mass, target_mass=target_mass, source_potential=source_potential, target_genes=target_genes)


epsilon = 0.05
geometry_weight = 4.0


def factors(embed):
    widened = embed.astype(jnp.float32)
    squares = jnp.sum(widened * widened, axis=0)
    unit_row = jnp.ones_like(squares)
    left_factor = jnp.concatenate([squares[None, :], unit_row[None, :], -2.0 * widened], axis=0)
    right_factor = jnp.concatenate([unit_row[None, :], squares[None, :], widened], axis=0)
    return left_factor, right_factor


def reference(source_embed, target_embed, source_expr, target_expr, current_plan, source_mass, target_mass, source_potential, target_genes):
    highest = lax.Precision.HIGHEST
    block_rows = math.gcd(NS, 2048)
    block_count = NS // block_rows
    left_src, right_src = factors(source_embed)
    left_tgt, right_tgt = factors(target_embed)
    plan_blocks = current_plan.reshape(block_count, block_rows, NT)

    def core_rows(plan_block):
        return jnp.dot(plan_block.astype(jnp.float32), right_tgt.T, precision=highest, preferred_element_type=jnp.float32)

    projected = lax.map(core_rows, plan_blocks).reshape(NS, RANK)
    core_matrix = jnp.dot(right_src, projected, precision=highest, preferred_element_type=jnp.float32) / (NS * NT)
    geometry_right = jnp.dot(core_matrix, left_tgt, precision=highest, preferred_element_type=jnp.float32)

    def cost_block(block_index):
        offset = (block_index * block_rows).astype(jnp.int32)
        expr_block = lax.dynamic_slice_in_dim(source_expr, offset, block_rows, 1)
        factor_block = lax.dynamic_slice_in_dim(left_src, offset, block_rows, 1)
        feature = jnp.dot(expr_block.T, target_expr, preferred_element_type=jnp.float32)
        geometry = jnp.dot(factor_block.T, geometry_right, precision=highest, preferred_element_type=jnp.float32)
        return -2.0 * (feature + geometry_weight * geometry)

    cost_tiles = lax.map(cost_block, jnp.arange(block_count, dtype=jnp.int32))
    log_src = jnp.log(source_mass).reshape(block_count, block_rows)
    log_tgt = jnp.log(target_mass)
    potential_src = source_potential.reshape(block_count, block_rows)
    potential_tgt = jnp.zeros((NT,), jnp.float32)
    for iteration in range(ITERS):
        def column_step(carry_pair, inputs):
            running_max, running_sum = carry_pair
            cost_piece, potential_piece = inputs
            scores = (potential_piece[:, None] - cost_piece) / epsilon
            maximum = jnp.maximum(running_max, jnp.max(scores, axis=0))
            running_sum = running_sum * jnp.exp(running_max - maximum) + jnp.sum(jnp.exp(scores - maximum[None, :]), axis=0)
            return (maximum, running_sum), None

        start_max = jnp.full((NT,), -jnp.inf, dtype=jnp.float32)
        start_sum = jnp.zeros((NT,), jnp.float32)
        (column_max, column_sum), unused = lax.scan(column_step, (start_max, start_sum), (cost_tiles, potential_src))
        potential_tgt = epsilon * log_tgt - epsilon * (column_max + jnp.log(column_sum))

        def row_step(cost_piece, current_tgt=potential_tgt):
            scores = (current_tgt[None, :] - cost_piece) / epsilon
            maximum = jnp.max(scores, axis=1)
            return maximum + jnp.log(jnp.sum(jnp.exp(scores - maximum[:, None]), axis=1))

        potential_src = epsilon * log_src - epsilon * lax.map(row_step, cost_tiles)

    def impute_block(pieces):
        cost_piece, potential_piece, mass_piece = pieces
        weights = jnp.exp((potential_piece[:, None] + potential_tgt[None, :] - cost_piece) / epsilon).astype(jnp.bfloat16)
        return jnp.dot(weights, target_genes, preferred_element_type=jnp.float32) / mass_piece[:, None]

    imputed = lax.map(impute_block, (cost_tiles, potential_src, source_mass.reshape(block_count, block_rows)))
    return imputed.reshape(NS, GENES).astype(jnp.bfloat16)
```

```python
import functools
import math

import jax
import jax.numpy as jnp
from jax import lax
from jax.experimental import pallas as pl
from jax.experimental.pallas import tpu as pltpu
from jax.sharding import PartitionSpec as P

EPSILON = 0.05
GEOMETRY_WEIGHT = 4.0
LOG2E = math.log2(math.e)
KAPPA = 2.0 * LOG2E / EPSILON
MESH = pl.DeviceIdType.MESH
F32 = jnp.float32
BF16 = jnp.bfloat16
TILES = 17
HIGHEST = lax.Precision.HIGHEST


def split3(value):
    high = value.astype(BF16)
    rest = value - high.astype(F32)
    middle = rest.astype(BF16)
    low = (rest - middle.astype(F32)).astype(BF16)
    return high, middle, low


def dot(a, b, dims):
    return lax.dot_general(a, b, (dims, ((), ())), preferred_element_type=F32)


def dot3(a, b, dims):
    high, middle, low = split3(a)
    return dot(high, b, dims) + (dot(middle, b, dims) + dot(low, b, dims))


def exact(a, b, dims):
    return lax.dot_general(a, b, (dims, ((), ())), precision=HIGHEST, preferred_element_type=F32)


def kernel(
    src_n, tgt_n, total_pairs, rows, step,
    es_ref, et_ref, xs_ref, xt_ref, plan_ref, ms_ref, mt_ref, fs_ref, genes_ref,
    out_ref,
    right, xf, lhs_rest, emb, expr, tmass, genes, partial, collected, core,
    rhs, yf, score, lse, gpot, colmax, colsum,
    tgt_send, tgt_recv, rs_send, rs_recv, ag_send, ag_recv, lse_send, lse_recv,
):
    n = src_n * tgt_n
    s = lax.axis_index("src")
    t = lax.axis_index("tgt")
    me = s * tgt_n + t
    cols = et_ref.shape[1]
    nt = cols * tgt_n
    local = es_ref.shape[1]
    lanes = nt // 128
    base = t * rows

    def place(linear):
        return (linear // tgt_n, linear % tgt_n)

    def owner(tile):
        return (tile, tile % 2) if tile < 16 else (0, 1)

    barrier = pltpu.get_barrier_semaphore()

    def greet(k, carry):
        pl.semaphore_signal(barrier, inc=1, device_id=place((me + k) % n), device_id_type=MESH)
        return carry

    lax.fori_loop(1, n, greet, 0)

    embed = es_ref[...]
    right[0:128, :] = embed
    wide = embed.astype(F32)
    q_src = jnp.sum(wide * wide, axis=0, keepdims=True)
    xf[...] = jnp.zeros_like(xf)
    xf[0:3, :] = jnp.ones((3, local), F32)

    def put(ref, value, spots):
        pieces = split3(value)
        for piece, places in zip(pieces, spots):
            for at in places:
                ref[at:at + 1, :] = piece.astype(F32)

    put(xf, q_src, ((3, 4, 5), (6, 7), (8,)))
    put(xf, 0.5 * fs_ref[...], ((9,), (10,), (11,)))
    put(xf, jnp.log2(ms_ref[...]), ((12,), (13,), (14,)))
    put(xf, ms_ref[...], ((15,), (16,), (17,)))
    right[128:160, :] = xf[...].astype(BF16)

    pl.semaphore_wait(barrier, n - 1)

    sent = []
    for d in range(1, tgt_n):
        peer = (s, (t + d) % tgt_n)
        for a, (ref, place_ref) in enumerate(
            ((et_ref, emb), (xt_ref, expr), (mt_ref, tmass), (genes_ref, genes))
        ):
            sent.append(
                pltpu.make_async_remote_copy(
                    src_ref=ref, dst_ref=place_ref.at[t],
                    send_sem=tgt_send.at[a, d - 1], recv_sem=tgt_recv.at[a, d - 1],
                    device_id=peer, device_id_type=MESH,
                )
            )
    for copy in sent:
        copy.start()
    emb[t] = et_ref[...]
    expr[t] = xt_ref[...]
    tmass[t] = mt_ref[...]
    genes[t] = genes_ref[...]

    here = dot(right[...], plan_ref[...], ((1,), (0,)))
    target = et_ref[...]
    target_wide = target.astype(F32)
    q_tgt = jnp.sum(target_wide * target_wide, axis=0, keepdims=True)
    by_e = here[0:128, :]
    by_one = here[128:129, :]
    by_q = here[131:132, :] + (here[134:135, :] + here[136:137, :])
    partial[0:16] = dot3(by_e, target, ((1,), (1,))).reshape(16, 8, 128)
    row = lax.broadcasted_iota(jnp.int32, (8, cols), 0)
    pair = jnp.where(row == 0, 1.0, jnp.where(row == 1, q_tgt, 0.0))
    sums = jnp.where(row == 2, by_one, jnp.where(row == 3, by_q, 0.0))
    border = exact(pair, by_e, ((1,), (1,))) + dot3(sums, target, ((1,), (1,)))
    scalar_rows = jnp.where(
        row == 4, by_one,
        jnp.where(row == 5, by_one * q_tgt, jnp.where(row == 6, by_q, jnp.where(row == 7, by_q * q_tgt, 0.0))),
    )
    border = border + jnp.sum(scalar_rows, axis=1, keepdims=True)
    partial[16] = border

    def to_owner(tile):
        return pltpu.make_async_remote_copy(
            src_ref=partial.at[tile], dst_ref=collected.at[me],
            send_sem=rs_send.at[tile], recv_sem=rs_recv,
            device_id=owner(tile), device_id_type=MESH,
        )

    def mine(tile):
        return (s == owner(tile)[0]) & (t == owner(tile)[1])

    for tile in range(TILES):
        @pl.when(jnp.logical_not(mine(tile)))
        def _():
            to_owner(tile).start()

    own_tile = jnp.where((s == 0) & (t == 1), 16, jnp.minimum(s, 15))
    owns = ((s < 16) & (t == s % 2)) | ((s == 0) & (t == 1))

    @pl.when(owns)
    def _():
        collected[me] = partial[own_tile]
        whole = collected.at[pl.ds(0, n - 1)]
        pltpu.make_async_remote_copy(
            src_ref=whole, dst_ref=whole, send_sem=ag_send, recv_sem=rs_recv,
            device_id=place((me + 1) % n), device_id_type=MESH,
        ).wait_recv()
        core[own_tile] = jnp.sum(collected[...], axis=0)

        def spread(k, carry):
            pltpu.make_async_remote_copy(
                src_ref=core.at[own_tile], dst_ref=core.at[own_tile],
                send_sem=ag_send, recv_sem=ag_recv.at[own_tile],
                device_id=place((me + k) % n), device_id_type=MESH,
            ).start()
            return carry

        lax.fori_loop(1, n, spread, 0)

    for copy in sent[0::4] + sent[1::4] + sent[2::4]:
        copy.wait_recv()

    for tile in range(TILES):
        @pl.when(jnp.logical_not(mine(tile)))
        def _():
            pltpu.make_async_remote_copy(
                src_ref=core.at[tile], dst_ref=core.at[tile],
                send_sem=ag_send, recv_sem=ag_recv.at[tile],
                device_id=place((me + 1) % n), device_id_type=MESH,
            ).wait_recv()

    middle = core[0:16].reshape(128, 128) / total_pairs
    edge = core[16] / total_pairs
    yf[...] = jnp.zeros_like(yf)
    yf[9:12, :] = jnp.ones((3, nt), F32)
    row8 = lax.broadcasted_iota(jnp.int32, (8, cols), 0)
    for block in range(tgt_n):
        at = slice(block * cols, (block + 1) * cols)
        e_t = emb[block]
        e_wide = e_t.astype(F32)
        q_t = jnp.sum(e_wide * e_wide, axis=0, keepdims=True)
        ends = jnp.where(row8 == 0, q_t, jnp.where(row8 == 1, 1.0, 0.0))
        g_e = -2.0 * dot3(middle, e_t, ((1,), (0,))) + exact(edge, ends, ((0,), (0,)))
        high, mid, low = split3((-2.0 * GEOMETRY_WEIGHT) * g_e)
        rhs[0:128, at] = expr[block]
        rhs[128:256, at] = high
        rhs[256:384, at] = mid
        rhs[384:512, at] = low
        g_x = -2.0 * dot3(edge, e_t, ((1,), (0,)))
        g_0 = g_x[2:3, :] + edge[4:5, 0:1] * q_t + edge[5:6, 0:1]
        g_1 = g_x[3:4, :] + edge[6:7, 0:1] * q_t + edge[7:8, 0:1]
        high, mid, low = [p.astype(F32) for p in split3(GEOMETRY_WEIGHT * g_1)]
        yf[0:1, at] = high
        yf[1:2, at] = mid
        yf[2:3, at] = low
        high, mid, low = [p.astype(F32) for p in split3(GEOMETRY_WEIGHT * g_0)]
        for spot, piece in zip(range(3, 9), (high, mid, low, high, mid, high)):
            yf[spot:spot + 1, at] = piece
    rhs[512:544, :] = yf[...].astype(BF16)

    def column_fold(values):
        top = jnp.max(values, axis=0, keepdims=True)
        before = colmax[...]
        now = jnp.maximum(before, top)
        colsum[...] = colsum[...] * jnp.exp2(before - now) + jnp.sum(
            jnp.exp2(values - now), axis=0, keepdims=True
        )
        colmax[...] = now

    def column_start():
        colmax[...] = jnp.full_like(colmax, -1e30)
        colsum[...] = jnp.zeros_like(colsum)

    def share(turn):
        held = colmax[...] + jnp.log2(colsum[...])
        for c in range(lanes):
            lse[turn, me, c:c + 1, :] = held[:, c * 128:(c + 1) * 128]

        def spread(k, carry):
            pltpu.make_async_remote_copy(
                src_ref=lse.at[turn, me], dst_ref=lse.at[turn, me],
                send_sem=lse_send.at[turn], recv_sem=lse_recv.at[turn],
                device_id=place((me + k) % n), device_id_type=MESH,
            ).start()
            return carry

        lax.fori_loop(1, n, spread, 0)
        whole = lse.at[turn, pl.ds(0, n - 1)]
        every = pltpu.make_async_remote_copy(
            src_ref=whole, dst_ref=whole,
            send_sem=lse_send.at[turn], recv_sem=lse_recv.at[turn],
            device_id=place((me + 1) % n), device_id_type=MESH,
        )
        every.wait_recv()
        parts = lse[turn]
        top = jnp.max(parts, axis=0)
        total = jnp.sum(jnp.exp2(parts - top[None]), axis=0)
        value = jnp.log2(tmass[...].reshape(lanes, 128)) - (top + jnp.log2(total))
        for c in range(lanes):
            gpot[0:1, c * 128:(c + 1) * 128] = value[c:c + 1, :]
        return every

    column_start()

    def scores(c, carry):
        src = pl.ds(pl.multiple_of(base + c * step, 128), step)
        e_s = right[0:128, src]
        a = jnp.concatenate([xs_ref[:, src], e_s], axis=0)
        b = jnp.concatenate([e_s, e_s], axis=0)
        tile = dot(a, rhs[0:256, :], ((0,), (0,)))
        tile = tile + dot(b, rhs[256:512, :], ((0,), (0,)))
        tile = tile + dot(right[128:160, src], rhs[512:544, :], ((0,), (0,)))
        tile = tile * KAPPA
        score[pl.ds(pl.multiple_of(c * step, 128), step), :] = tile
        column_fold(tile)
        return carry

    lax.fori_loop(0, rows // step, scores, 0)
    first = share(0)

    pick = lax.broadcasted_iota(jnp.int32, (32, 256), 0)
    side = lax.broadcasted_iota(jnp.int32, (32, 256), 1) // 128
    select = jnp.where(
        (pick >= 12 + 3 * side) & (pick < 15 + 3 * side), 1.0, 0.0
    ).astype(BF16)

    def source_columns(c):
        src = pl.ds(pl.multiple_of(base + c * step, 128), step)
        both = dot(right[128:160, src], select, ((0,), (0,)))
        return both[:, 0:1], both[:, 128:129]

    column_start()

    def middle_pass(c, carry):
        tile = score[pl.ds(pl.multiple_of(c * step, 128), step), :]
        log_mass, unused = source_columns(c)
        a = tile + gpot[...]
        top = jnp.max(a, axis=1, keepdims=True)
        total = jnp.sum(jnp.exp2(a - top), axis=1, keepdims=True)
        moved = log_mass - (top + jnp.log2(total))
        column_fold(tile + moved)
        return carry

    lax.fori_loop(0, rows // step, middle_pass, 0)
    second = share(1)

    for copy in sent[3::4]:
        copy.wait_recv()
    gene_rows = genes[...].reshape(nt, genes.shape[2])

    def last_pass(c, carry):
        at = pl.ds(pl.multiple_of(c * step, 128), step)
        log_mass, mass = source_columns(c)
        a = score[at, :] + gpot[...]
        top = jnp.max(a, axis=1, keepdims=True)
        p = jnp.exp2(a - top)
        total = jnp.sum(p, axis=1, keepdims=True)
        potential = log_mass - (top + jnp.log2(total))
        numerator = dot(p.astype(BF16), gene_rows, ((1,), (0,)))
        out_ref[at, :] = (numerator * (jnp.exp2(potential + top) / mass)).astype(BF16)
        return carry

    lax.fori_loop(0, rows // step, last_pass, 0)

    for copy in sent:
        copy.wait_send()
    for tile in range(TILES):
        @pl.when(jnp.logical_not(mine(tile)))
        def _():
            to_owner(tile).wait_send()

    @pl.when(owns)
    def _():
        whole = collected.at[pl.ds(0, n - 1)]
        pltpu.make_async_remote_copy(
            src_ref=whole, dst_ref=whole, send_sem=ag_send, recv_sem=rs_recv,
            device_id=place((me + 1) % n), device_id_type=MESH,
        ).wait_send()

    first.wait_send()
    second.wait_send()


def shards(src_n, tgt_n, es, et, xs, xt, plan, ms, mt, fs, genes):
    n = src_n * tgt_n
    local = es.shape[1]
    cols = et.shape[1]
    nt = cols * tgt_n
    rows = local // tgt_n
    step = min(rows, 256) if nt <= 1024 else 128
    total_pairs = float(local * src_n * nt)
    gene_count = genes.shape[1]
    body = functools.partial(kernel, src_n, tgt_n, total_pairs, rows, step)
    vmem = pl.BlockSpec(memory_space=pltpu.VMEM)
    dma = pltpu.SemaphoreType.DMA
    return pl.pallas_call(
        body,
        out_shape=jax.ShapeDtypeStruct((rows, gene_count), BF16),
        in_specs=[vmem] * 9,
        out_specs=vmem,
        scratch_shapes=[
            pltpu.VMEM((160, local), BF16),
            pltpu.VMEM((32, local), F32),
            pltpu.VMEM((8, 128), F32),
            pltpu.VMEM((tgt_n, 128, cols), BF16),
            pltpu.VMEM((tgt_n, 128, cols), BF16),
            pltpu.VMEM((tgt_n, cols // 128, 128), F32),
            pltpu.VMEM((tgt_n, cols, gene_count), BF16),
            pltpu.VMEM((TILES, 8, 128), F32),
            pltpu.VMEM((n, 8, 128), F32),
            pltpu.VMEM((TILES, 8, 128), F32),
            pltpu.VMEM((544, nt), BF16),
            pltpu.VMEM((32, nt), F32),
            pltpu.VMEM((rows, nt), F32),
            pltpu.VMEM((2, n, nt // 128, 128), F32),
            pltpu.VMEM((1, nt), F32),
            pltpu.VMEM((1, nt), F32),
            pltpu.VMEM((1, nt), F32),
            dma((4, tgt_n - 1)),
            dma((4, tgt_n - 1)),
            dma((TILES,)),
            dma,
            dma,
            dma((TILES,)),
            dma((2,)),
            dma((2,)),
        ],
        compiler_params=pltpu.CompilerParams(
            collective_id=0, has_side_effects=True, vmem_limit_bytes=56 * 1024 * 1024
        ),
    )(
        es, et, xs, xt, plan,
        ms.reshape(1, local), mt.reshape(cols // 128, 128), fs.reshape(1, local), genes,
    )


def solution(mesh):
    src_n = mesh.shape["src"]
    tgt_n = mesh.shape["tgt"]
    return jax.shard_map(
        functools.partial(shards, src_n, tgt_n),
        mesh=mesh,
        in_specs=(
            P(None, "src"),
            P(None, "tgt"),
            P(None, "src"),
            P(None, "tgt"),
            P("src", "tgt"),
            P("src"),
            P("tgt"),
            P("src"),
            P("tgt", None),
        ),
        out_specs=P(("src", "tgt"), None),
        check_vma=False,
    )
```

```python
import functools
import math

import jax
import jax.numpy as jnp
from jax import lax
from jax.experimental import pallas as pl
from jax.experimental.pallas import tpu as pltpu
from jax.sharding import PartitionSpec as P

EPSILON = 0.05
GEOMETRY_WEIGHT = 4.0
LOG2E = math.log2(math.e)
KAPPA = 2.0 * LOG2E / EPSILON
MESH = pl.DeviceIdType.MESH
F32 = jnp.float32
BF16 = jnp.bfloat16
TILES = 17
CHUNKS = 4
HIGHEST = lax.Precision.HIGHEST


def split3(value):
    high = value.astype(BF16)
    rest = value - high.astype(F32)
    middle = rest.astype(BF16)
    low = (rest - middle.astype(F32)).astype(BF16)
    return high, middle, low


def dot(a, b, dims):
    return lax.dot_general(a, b, (dims, ((), ())), preferred_element_type=F32)


def dot3(a, b, dims):
    high, middle, low = split3(a)
    return dot(high, b, dims) + (dot(middle, b, dims) + dot(low, b, dims))


def exact(a, b, dims):
    return lax.dot_general(a, b, (dims, ((), ())), precision=HIGHEST, preferred_element_type=F32)


def kernel(
    src_n, tgt_n, total_pairs, rows, step,
    es_ref, et_ref, xs_ref, xt_ref, plan_ref, ms_ref, mt_ref, fs_ref, genes_ref,
    out_ref,
    right, xf, plan, xs, emb, expr, tmass, genes, partial, collected, core,
    rhs, yf, score, near, far, gpot, colmax, colsum,
    in_sem, tgt_send, tgt_recv, fw_send, fw_recv, rs_send, rs_recv, ag_send, ag_recv,
    near_send, near_recv, far_send, far_recv,
):
    n = src_n * tgt_n
    s = lax.axis_index("src")
    t = lax.axis_index("tgt")
    me = s * tgt_n + t
    cols = et_ref.shape[1]
    nt = cols * tgt_n
    local = es_ref.shape[1]
    lanes = nt // 128
    base = t * rows

    def place(linear):
        return (linear // tgt_n, linear % tgt_n)

    def owner(tile):
        return (tile, tile % 2) if tile < 16 else (0, 1)

    barrier = pltpu.get_barrier_semaphore()

    def greet(k, carry):
        pl.semaphore_signal(barrier, inc=1, device_id=place((me + k) % n), device_id_type=MESH)
        return carry

    lax.fori_loop(1, n, greet, 0)

    plan_step = local // CHUNKS
    fetch_embed = pltpu.make_async_copy(es_ref, right.at[0:128], in_sem.at[0])
    fetch_plan = [
        pltpu.make_async_copy(
            plan_ref.at[c * plan_step:(c + 1) * plan_step],
            plan.at[c * plan_step:(c + 1) * plan_step], in_sem.at[3 + c],
        )
        for c in range(CHUNKS)
    ]
    fetch_expr = pltpu.make_async_copy(
        xs_ref.at[:, pl.ds(pl.multiple_of(base, 128), rows)], xs, in_sem.at[1]
    )
    fetch_genes = pltpu.make_async_copy(genes_ref, genes.at[t], in_sem.at[2])
    for copy in [fetch_embed] + fetch_plan + [fetch_expr, fetch_genes]:
        copy.start()
    fetch_embed.wait()

    wide = right[0:128, :].astype(F32)
    q_src = jnp.sum(wide * wide, axis=0, keepdims=True)
    xf[...] = jnp.zeros_like(xf)
    xf[0:3, :] = jnp.ones((3, local), F32)

    def put(ref, value, spots):
        pieces = split3(value)
        for piece, places in zip(pieces, spots):
            for at in places:
                ref[at:at + 1, :] = piece.astype(F32)

    put(xf, q_src, ((3, 4, 5), (6, 7), (8,)))
    put(xf, 0.5 * fs_ref[...], ((9,), (10,), (11,)))
    put(xf, jnp.log2(ms_ref[...]), ((12,), (13,), (14,)))
    put(xf, ms_ref[...], ((15,), (16,), (17,)))
    right[128:160, :] = xf[...].astype(BF16)

    pl.semaphore_wait(barrier, n - 1)

    half = s % 2
    sibling = (s + 1 - 2 * half, t)

    def part(size):
        return pl.ds(pl.multiple_of(half * (size // 2), size // 2), size // 2)

    emb_part, gene_part = part(128), part(cols)
    across, along = [], []
    for d in range(1, tgt_n):
        peer = (s, (t + d) % tgt_n)
        other = (t + tgt_n - d) % tgt_n
        for a, (ref, held, piece) in enumerate(
            ((et_ref, emb, emb_part), (xt_ref, expr, emb_part), (genes.at[t], genes, gene_part))
        ):
            across.append(
                pltpu.make_async_remote_copy(
                    src_ref=ref.at[piece], dst_ref=held.at[t, piece],
                    send_sem=tgt_send.at[a, d - 1], recv_sem=tgt_recv.at[a, d - 1],
                    device_id=peer, device_id_type=MESH,
                )
            )
            along.append(
                pltpu.make_async_remote_copy(
                    src_ref=held.at[other, piece], dst_ref=held.at[other, piece],
                    send_sem=fw_send.at[a, d - 1], recv_sem=fw_recv.at[a, d - 1],
                    device_id=sibling, device_id_type=MESH,
                )
            )
    masses = [
        pltpu.make_async_remote_copy(
            src_ref=mt_ref, dst_ref=tmass.at[t],
            send_sem=tgt_send.at[3, d - 1], recv_sem=tgt_recv.at[3, d - 1],
            device_id=(s, (t + d) % tgt_n), device_id_type=MESH,
        )
        for d in range(1, tgt_n)
    ]
    for copy in across[0::3] + across[1::3] + masses:
        copy.start()
    emb[t] = et_ref[...]
    expr[t] = xt_ref[...]
    tmass[t] = mt_ref[...]

    here = 0.0
    for c in range(CHUNKS):
        fetch_plan[c].wait()
        at = slice(c * plan_step, (c + 1) * plan_step)
        here = here + dot(right[:, at], plan[at, :], ((1,), (0,)))
    target = et_ref[...]
    target_wide = target.astype(F32)
    q_tgt = jnp.sum(target_wide * target_wide, axis=0, keepdims=True)
    by_e = here[0:128, :]
    by_one = here[128:129, :]
    by_q = here[131:132, :] + (here[134:135, :] + here[136:137, :])
    partial[0:16] = dot3(by_e, target, ((1,), (1,))).reshape(16, 8, 128)
    row = lax.broadcasted_iota(jnp.int32, (8, cols), 0)
    pair = jnp.where(row == 0, 1.0, jnp.where(row == 1, q_tgt, 0.0))
    sums = jnp.where(row == 2, by_one, jnp.where(row == 3, by_q, 0.0))
    border = exact(pair, by_e, ((1,), (1,))) + dot3(sums, target, ((1,), (1,)))
    scalar_rows = jnp.where(
        row == 4, by_one,
        jnp.where(row == 5, by_one * q_tgt, jnp.where(row == 6, by_q, jnp.where(row == 7, by_q * q_tgt, 0.0))),
    )
    border = border + jnp.sum(scalar_rows, axis=1, keepdims=True)
    partial[16] = border

    def to_owner(tile):
        return pltpu.make_async_remote_copy(
            src_ref=partial.at[tile], dst_ref=collected.at[me],
            send_sem=rs_send.at[tile], recv_sem=rs_recv,
            device_id=owner(tile), device_id_type=MESH,
        )

    def mine(tile):
        return (s == owner(tile)[0]) & (t == owner(tile)[1])

    for tile in range(TILES):
        @pl.when(jnp.logical_not(mine(tile)))
        def _():
            to_owner(tile).start()

    for copy, onward in list(zip(across, along))[0::3] + list(zip(across, along))[1::3]:
        copy.wait_recv()
        onward.start()

    own_tile = jnp.where((s == 0) & (t == 1), 16, jnp.minimum(s, 15))
    owns = ((s < 16) & (t == s % 2)) | ((s == 0) & (t == 1))

    @pl.when(owns)
    def _():
        collected[me] = partial[own_tile]
        whole = collected.at[pl.ds(0, n - 1)]
        pltpu.make_async_remote_copy(
            src_ref=whole, dst_ref=whole, send_sem=ag_send, recv_sem=rs_recv,
            device_id=place((me + 1) % n), device_id_type=MESH,
        ).wait_recv()
        core[own_tile] = jnp.sum(collected[...], axis=0)

        def spread(k, carry):
            pltpu.make_async_remote_copy(
                src_ref=core.at[own_tile], dst_ref=core.at[own_tile],
                send_sem=ag_send, recv_sem=ag_recv.at[own_tile],
                device_id=place((me + k) % n), device_id_type=MESH,
            ).start()
            return carry

        lax.fori_loop(1, n, spread, 0)

    for copy in along[0::3] + along[1::3] + masses:
        copy.wait_recv()

    for tile in range(TILES):
        @pl.when(jnp.logical_not(mine(tile)))
        def _():
            pltpu.make_async_remote_copy(
                src_ref=core.at[tile], dst_ref=core.at[tile],
                send_sem=ag_send, recv_sem=ag_recv.at[tile],
                device_id=place((me + 1) % n), device_id_type=MESH,
            ).wait_recv()

    fetch_genes.wait()
    for copy in across[2::3]:
        copy.start()

    middle = core[0:16].reshape(128, 128) / total_pairs
    edge = core[16] / total_pairs
    yf[...] = jnp.zeros_like(yf)
    yf[9:12, :] = jnp.ones((3, nt), F32)
    row8 = lax.broadcasted_iota(jnp.int32, (8, cols), 0)
    for block in range(tgt_n):
        at = slice(block * cols, (block + 1) * cols)
        e_t = emb[block]
        e_wide = e_t.astype(F32)
        q_t = jnp.sum(e_wide * e_wide, axis=0, keepdims=True)
        ends = jnp.where(row8 == 0, q_t, jnp.where(row8 == 1, 1.0, 0.0))
        g_e = -2.0 * dot3(middle, e_t, ((1,), (0,))) + exact(edge, ends, ((0,), (0,)))
        high, mid, low = split3((-2.0 * GEOMETRY_WEIGHT) * g_e)
        rhs[0:128, at] = expr[block]
        rhs[128:256, at] = high
        rhs[256:384, at] = mid
        rhs[384:512, at] = low
        g_x = -2.0 * dot3(edge, e_t, ((1,), (0,)))
        g_0 = g_x[2:3, :] + edge[4:5, 0:1] * q_t + edge[5:6, 0:1]
        g_1 = g_x[3:4, :] + edge[6:7, 0:1] * q_t + edge[7:8, 0:1]
        high, mid, low = [p.astype(F32) for p in split3(GEOMETRY_WEIGHT * g_1)]
        yf[0:1, at] = high
        yf[1:2, at] = mid
        yf[2:3, at] = low
        high, mid, low = [p.astype(F32) for p in split3(GEOMETRY_WEIGHT * g_0)]
        for spot, piece in zip(range(3, 9), (high, mid, low, high, mid, high)):
            yf[spot:spot + 1, at] = piece
    rhs[512:544, :] = yf[...].astype(BF16)

    def column_fold(values):
        top = jnp.max(values, axis=0, keepdims=True)
        before = colmax[...]
        now = jnp.maximum(before, top)
        colsum[...] = colsum[...] * jnp.exp2(before - now) + jnp.sum(
            jnp.exp2(values - now), axis=0, keepdims=True
        )
        colmax[...] = now

    def column_start():
        colmax[...] = jnp.full_like(colmax, -1e30)
        colsum[...] = jnp.zeros_like(colsum)

    group = 4 * tgt_n
    rank = me % group
    level = me // group
    first_near = level * group

    def joined(parts):
        top = jnp.max(parts, axis=0)
        return top, jnp.sum(jnp.exp2(parts - top[None]), axis=0)

    def exchange(slots, slot, count, send_sem, recv_sem, peer):
        for k in range(1, count):
            pltpu.make_async_remote_copy(
                src_ref=slots.at[slot], dst_ref=slots.at[slot],
                send_sem=send_sem, recv_sem=recv_sem,
                device_id=peer(k), device_id_type=MESH,
            ).start()
        whole = slots.at[pl.ds(0, count - 1)]
        every = pltpu.make_async_remote_copy(
            src_ref=whole, dst_ref=whole, send_sem=send_sem, recv_sem=recv_sem,
            device_id=peer(1), device_id_type=MESH,
        )
        every.wait_recv()
        return every

    def share(turn):
        held = colmax[...] + jnp.log2(colsum[...])
        for c in range(lanes):
            near[turn, rank, c:c + 1, :] = held[:, c * 128:(c + 1) * 128]
        close = exchange(
            near.at[turn], rank, group, near_send.at[turn], near_recv.at[turn],
            lambda k: place(first_near + (rank + k) % group),
        )
        top, total = joined(near[turn])
        far[turn, level] = top + jnp.log2(total)
        wide_range = exchange(
            far.at[turn], level, n // group, far_send.at[turn], far_recv.at[turn],
            lambda k: place((me + k * group) % n),
        )
        top, total = joined(far[turn])
        value = jnp.log2(tmass[...].reshape(lanes, 128)) - (top + jnp.log2(total))
        for c in range(lanes):
            gpot[0:1, c * 128:(c + 1) * 128] = value[c:c + 1, :]
        return close, wide_range

    fetch_expr.wait()

    column_start()

    def scores(c, carry):
        src = pl.ds(pl.multiple_of(base + c * step, 128), step)
        e_s = right[0:128, src]
        a = jnp.concatenate([xs[:, pl.ds(pl.multiple_of(c * step, 128), step)], e_s], axis=0)
        b = jnp.concatenate([e_s, e_s], axis=0)
        tile = dot(a, rhs[0:256, :], ((0,), (0,)))
        tile = tile + dot(b, rhs[256:512, :], ((0,), (0,)))
        tile = tile + dot(right[128:160, src], rhs[512:544, :], ((0,), (0,)))
        tile = tile * KAPPA
        score[pl.ds(pl.multiple_of(c * step, 128), step), :] = tile
        column_fold(tile)
        return carry

    lax.fori_loop(0, rows // step, scores, 0)
    first = share(0)
    for copy, onward in list(zip(across, along))[2::3]:
        copy.wait_recv()
        onward.start()

    pick = lax.broadcasted_iota(jnp.int32, (32, 256), 0)
    side = lax.broadcasted_iota(jnp.int32, (32, 256), 1) // 128
    select = jnp.where(
        (pick >= 12 + 3 * side) & (pick < 15 + 3 * side), 1.0, 0.0
    ).astype(BF16)

    def source_columns(c):
        src = pl.ds(pl.multiple_of(base + c * step, 128), step)
        both = dot(right[128:160, src], select, ((0,), (0,)))
        return both[:, 0:1], both[:, 128:129]

    column_start()

    def middle_pass(c, carry):
        tile = score[pl.ds(pl.multiple_of(c * step, 128), step), :]
        log_mass, unused = source_columns(c)
        a = tile + gpot[...]
        top = jnp.max(a, axis=1, keepdims=True)
        total = jnp.sum(jnp.exp2(a - top), axis=1, keepdims=True)
        moved = log_mass - (top + jnp.log2(total))
        column_fold(tile + moved)
        return carry

    lax.fori_loop(0, rows // step, middle_pass, 0)
    second = share(1)

    for copy in along[2::3]:
        copy.wait_recv()
    gene_rows = genes[...].reshape(nt, genes.shape[2])

    def last_pass(c, carry):
        at = pl.ds(pl.multiple_of(c * step, 128), step)
        log_mass, mass = source_columns(c)
        a = score[at, :] + gpot[...]
        top = jnp.max(a, axis=1, keepdims=True)
        p = jnp.exp2(a - top)
        total = jnp.sum(p, axis=1, keepdims=True)
        potential = log_mass - (top + jnp.log2(total))
        numerator = dot(p.astype(BF16), gene_rows, ((1,), (0,)))
        out_ref[at, :] = (numerator * (jnp.exp2(potential + top) / mass)).astype(BF16)
        return carry

    lax.fori_loop(0, rows // step, last_pass, 0)

    for copy in across + along + masses + list(first) + list(second):
        copy.wait_send()
    for tile in range(TILES):
        @pl.when(jnp.logical_not(mine(tile)))
        def _():
            to_owner(tile).wait_send()

    @pl.when(owns)
    def _():
        whole = collected.at[pl.ds(0, n - 1)]
        pltpu.make_async_remote_copy(
            src_ref=whole, dst_ref=whole, send_sem=ag_send, recv_sem=rs_recv,
            device_id=place((me + 1) % n), device_id_type=MESH,
        ).wait_send()


def shards(src_n, tgt_n, es, et, xs, xt, plan, ms, mt, fs, genes):
    n = src_n * tgt_n
    local = es.shape[1]
    cols = et.shape[1]
    nt = cols * tgt_n
    rows = local // tgt_n
    step = min(rows, 256) if nt <= 1024 else 128
    total_pairs = float(local * src_n * nt)
    gene_count = genes.shape[1]
    body = functools.partial(kernel, src_n, tgt_n, total_pairs, rows, step)
    anywhere = pl.BlockSpec(memory_space=pl.ANY)
    vmem = pl.BlockSpec(memory_space=pltpu.VMEM)
    dma = pltpu.SemaphoreType.DMA
    return pl.pallas_call(
        body,
        out_shape=jax.ShapeDtypeStruct((rows, gene_count), BF16),
        in_specs=[anywhere, vmem, anywhere, vmem, anywhere, vmem, vmem, vmem, anywhere],
        out_specs=vmem,
        scratch_shapes=[
            pltpu.VMEM((160, local), BF16),
            pltpu.VMEM((32, local), F32),
            pltpu.VMEM((local, cols), BF16),
            pltpu.VMEM((128, rows), BF16),
            pltpu.VMEM((tgt_n, 128, cols), BF16),
            pltpu.VMEM((tgt_n, 128, cols), BF16),
            pltpu.VMEM((tgt_n, cols // 128, 128), F32),
            pltpu.VMEM((tgt_n, cols, gene_count), BF16),
            pltpu.VMEM((TILES, 8, 128), F32),
            pltpu.VMEM((n, 8, 128), F32),
            pltpu.VMEM((TILES, 8, 128), F32),
            pltpu.VMEM((544, nt), BF16),
            pltpu.VMEM((32, nt), F32),
            pltpu.VMEM((rows, nt), F32),
            pltpu.VMEM((2, 4 * tgt_n, nt // 128, 128), F32),
            pltpu.VMEM((2, src_n // 4, nt // 128, 128), F32),
            pltpu.VMEM((1, nt), F32),
            pltpu.VMEM((1, nt), F32),
            pltpu.VMEM((1, nt), F32),
            dma((3 + CHUNKS,)),
            dma((4, tgt_n - 1)),
            dma((4, tgt_n - 1)),
            dma((3, tgt_n - 1)),
            dma((3, tgt_n - 1)),
            dma((TILES,)),
            dma,
            dma,
            dma((TILES,)),
            dma((2,)),
            dma((2,)),
            dma((2,)),
            dma((2,)),
        ],
        compiler_params=pltpu.CompilerParams(
            collective_id=0, has_side_effects=True, vmem_limit_bytes=56 * 1024 * 1024
        ),
    )(
        es, et, xs, xt, plan,
        ms.reshape(1, local), mt.reshape(cols // 128, 128), fs.reshape(1, local), genes,
    )


def solution(mesh):
    src_n = mesh.shape["src"]
    tgt_n = mesh.shape["tgt"]
    return jax.shard_map(
        functools.partial(shards, src_n, tgt_n),
        mesh=mesh,
        in_specs=(
            P(None, "src"),
            P(None, "tgt"),
            P(None, "src"),
            P(None, "tgt"),
            P("src", "tgt"),
            P("src"),
            P("tgt"),
            P("src"),
            P("tgt", None),
        ),
        out_specs=P(("src", "tgt"), None),
        check_vma=False,
    )
```

```python
import functools
import math

import jax
import jax.numpy as jnp
from jax import lax
from jax.experimental import pallas as pl
from jax.experimental.pallas import tpu as pltpu
from jax.sharding import PartitionSpec as P

EPSILON = 0.05
GEOMETRY_WEIGHT = 4.0
LOG2E = math.log2(math.e)
KAPPA = 2.0 * LOG2E / EPSILON
MESH = pl.DeviceIdType.MESH
F32 = jnp.float32
BF16 = jnp.bfloat16
TILES = 17
CHUNKS = 4
HIGHEST = lax.Precision.HIGHEST


def split3(value):
    high = value.astype(BF16)
    rest = value - high.astype(F32)
    middle = rest.astype(BF16)
    low = (rest - middle.astype(F32)).astype(BF16)
    return high, middle, low


def dot(a, b, dims):
    return lax.dot_general(a, b, (dims, ((), ())), preferred_element_type=F32)


def dot3(a, b, dims):
    high, middle, low = split3(a)
    return dot(high, b, dims) + (dot(middle, b, dims) + dot(low, b, dims))


def exact(a, b, dims):
    return lax.dot_general(a, b, (dims, ((), ())), precision=HIGHEST, preferred_element_type=F32)


def kernel(
    src_n, tgt_n, total_pairs, rows, step,
    es_ref, et_ref, xs_ref, xt_ref, plan_ref, ms_ref, mt_ref, fs_ref, genes_ref,
    out_ref,
    right, xf, plan, xs, emb, expr, tmass, genes, partial, collected, core,
    rhs, yf, score, near, far, gpot, colmax, colsum,
    in_sem, tgt_send, tgt_recv, fw_send, fw_recv, rs_send, rs_recv, ag_send, ag_recv,
    near_send, near_recv, far_send, far_recv,
):
    n = src_n * tgt_n
    s = lax.axis_index("src")
    t = lax.axis_index("tgt")
    me = s * tgt_n + t
    cols = et_ref.shape[1]
    nt = cols * tgt_n
    local = es_ref.shape[1]
    lanes = nt // 128
    base = t * rows

    def place(linear):
        return (linear // tgt_n, linear % tgt_n)

    def owner(tile):
        return (tile, tile % 2) if tile < 16 else (0, 1)

    barrier = pltpu.get_barrier_semaphore()

    def greet(k, carry):
        pl.semaphore_signal(barrier, inc=1, device_id=place((me + k) % n), device_id_type=MESH)
        return carry

    lax.fori_loop(1, n, greet, 0)

    plan_step = local // CHUNKS
    fetch_embed = pltpu.make_async_copy(es_ref, right.at[0:128], in_sem.at[0])
    fetch_plan = [
        pltpu.make_async_copy(
            plan_ref.at[c * plan_step:(c + 1) * plan_step],
            plan.at[c * plan_step:(c + 1) * plan_step], in_sem.at[3 + c],
        )
        for c in range(CHUNKS)
    ]
    fetch_expr = pltpu.make_async_copy(
        xs_ref.at[:, pl.ds(pl.multiple_of(base, 128), rows)], xs, in_sem.at[1]
    )
    fetch_genes = pltpu.make_async_copy(genes_ref, genes.at[t], in_sem.at[2])
    for copy in [fetch_embed] + fetch_plan + [fetch_expr, fetch_genes]:
        copy.start()
    fetch_embed.wait()

    wide = right[0:128, :].astype(F32)
    q_src = jnp.sum(wide * wide, axis=0, keepdims=True)
    xf[...] = jnp.zeros_like(xf)
    xf[0:3, :] = jnp.ones((3, local), F32)

    def put(ref, value, spots):
        pieces = split3(value)
        for piece, places in zip(pieces, spots):
            for at in places:
                ref[at:at + 1, :] = piece.astype(F32)

    put(xf, q_src, ((3, 4, 5), (6, 7), (8,)))
    put(xf, 0.5 * fs_ref[...], ((9,), (10,), (11,)))
    put(xf, jnp.log2(ms_ref[...]), ((12,), (13,), (14,)))
    put(xf, ms_ref[...], ((15,), (16,), (17,)))
    right[128:160, :] = xf[...].astype(BF16)

    pl.semaphore_wait(barrier, n - 1)

    half = s % 2
    sibling = (s + 1 - 2 * half, t)

    def part(size):
        return pl.ds(pl.multiple_of(half * (size // 2), size // 2), size // 2)

    emb_part, gene_part = part(128), part(cols)
    across, along = [], []
    for d in range(1, tgt_n):
        peer = (s, (t + d) % tgt_n)
        other = (t + tgt_n - d) % tgt_n
        for a, (ref, held, piece) in enumerate(
            ((et_ref, emb, emb_part), (xt_ref, expr, emb_part), (genes.at[t], genes, gene_part))
        ):
            across.append(
                pltpu.make_async_remote_copy(
                    src_ref=ref.at[piece], dst_ref=held.at[t, piece],
                    send_sem=tgt_send.at[a, d - 1], recv_sem=tgt_recv.at[a, d - 1],
                    device_id=peer, device_id_type=MESH,
                )
            )
            along.append(
                pltpu.make_async_remote_copy(
                    src_ref=held.at[other, piece], dst_ref=held.at[other, piece],
                    send_sem=fw_send.at[a, d - 1], recv_sem=fw_recv.at[a, d - 1],
                    device_id=sibling, device_id_type=MESH,
                )
            )
    masses = [
        pltpu.make_async_remote_copy(
            src_ref=mt_ref, dst_ref=tmass.at[t],
            send_sem=tgt_send.at[3, d - 1], recv_sem=tgt_recv.at[3, d - 1],
            device_id=(s, (t + d) % tgt_n), device_id_type=MESH,
        )
        for d in range(1, tgt_n)
    ]
    for copy in across[0::3] + across[1::3] + masses:
        copy.start()
    emb[t] = et_ref[...]
    expr[t] = xt_ref[...]
    tmass[t] = mt_ref[...]

    here = 0.0
    for c in range(CHUNKS):
        fetch_plan[c].wait()
        at = slice(c * plan_step, (c + 1) * plan_step)
        here = here + dot(right[:, at], plan[at, :], ((1,), (0,)))
    target = et_ref[...]
    target_wide = target.astype(F32)
    q_tgt = jnp.sum(target_wide * target_wide, axis=0, keepdims=True)
    by_e = here[0:128, :]
    by_one = here[128:129, :]
    by_q = here[131:132, :] + (here[134:135, :] + here[136:137, :])
    partial[0:16] = dot3(by_e, target, ((1,), (1,))).reshape(16, 8, 128)
    row = lax.broadcasted_iota(jnp.int32, (8, cols), 0)
    pair = jnp.where(row == 0, 1.0, jnp.where(row == 1, q_tgt, 0.0))
    sums = jnp.where(row == 2, by_one, jnp.where(row == 3, by_q, 0.0))
    border = exact(pair, by_e, ((1,), (1,))) + dot3(sums, target, ((1,), (1,)))
    scalar_rows = jnp.where(
        row == 4, by_one,
        jnp.where(row == 5, by_one * q_tgt, jnp.where(row == 6, by_q, jnp.where(row == 7, by_q * q_tgt, 0.0))),
    )
    border = border + jnp.sum(scalar_rows, axis=1, keepdims=True)
    partial[16] = border

    def to_owner(tile):
        return pltpu.make_async_remote_copy(
            src_ref=partial.at[tile], dst_ref=collected.at[me],
            send_sem=rs_send.at[tile], recv_sem=rs_recv,
            device_id=owner(tile), device_id_type=MESH,
        )

    def mine(tile):
        return (s == owner(tile)[0]) & (t == owner(tile)[1])

    for tile in range(TILES):
        @pl.when(jnp.logical_not(mine(tile)))
        def _():
            to_owner(tile).start()

    for copy, onward in list(zip(across, along))[0::3] + list(zip(across, along))[1::3]:
        copy.wait_recv()
        onward.start()

    own_tile = jnp.where((s == 0) & (t == 1), 16, jnp.minimum(s, 15))
    owns = ((s < 16) & (t == s % 2)) | ((s == 0) & (t == 1))

    @pl.when(owns)
    def _():
        collected[me] = partial[own_tile]
        whole = collected.at[pl.ds(0, n - 1)]
        pltpu.make_async_remote_copy(
            src_ref=whole, dst_ref=whole, send_sem=ag_send, recv_sem=rs_recv,
            device_id=place((me + 1) % n), device_id_type=MESH,
        ).wait_recv()
        core[own_tile] = jnp.sum(collected[...], axis=0)

        def spread(k, carry):
            pltpu.make_async_remote_copy(
                src_ref=core.at[own_tile], dst_ref=core.at[own_tile],
                send_sem=ag_send, recv_sem=ag_recv.at[own_tile],
                device_id=place((me + k) % n), device_id_type=MESH,
            ).start()
            return carry

        lax.fori_loop(1, n, spread, 0)

    for copy in along[0::3] + along[1::3] + masses:
        copy.wait_recv()

    for tile in range(TILES):
        @pl.when(jnp.logical_not(mine(tile)))
        def _():
            pltpu.make_async_remote_copy(
                src_ref=core.at[tile], dst_ref=core.at[tile],
                send_sem=ag_send, recv_sem=ag_recv.at[tile],
                device_id=place((me + 1) % n), device_id_type=MESH,
            ).wait_recv()

    fetch_genes.wait()
    for copy in across[2::3]:
        copy.start()

    middle = core[0:16].reshape(128, 128) / total_pairs
    edge = core[16] / total_pairs
    yf[...] = jnp.zeros_like(yf)
    yf[9:12, :] = jnp.ones((3, nt), F32)
    row8 = lax.broadcasted_iota(jnp.int32, (8, cols), 0)
    for block in range(tgt_n):
        at = slice(block * cols, (block + 1) * cols)
        e_t = emb[block]
        e_wide = e_t.astype(F32)
        q_t = jnp.sum(e_wide * e_wide, axis=0, keepdims=True)
        ends = jnp.where(row8 == 0, q_t, jnp.where(row8 == 1, 1.0, 0.0))
        g_e = -2.0 * dot3(middle, e_t, ((1,), (0,))) + exact(edge, ends, ((0,), (0,)))
        high, mid, low = split3((-2.0 * GEOMETRY_WEIGHT) * g_e)
        rhs[0:128, at] = expr[block]
        rhs[128:256, at] = high
        rhs[256:384, at] = mid
        rhs[384:512, at] = low
        g_x = -2.0 * dot3(edge, e_t, ((1,), (0,)))
        g_0 = g_x[2:3, :] + edge[4:5, 0:1] * q_t + edge[5:6, 0:1]
        g_1 = g_x[3:4, :] + edge[6:7, 0:1] * q_t + edge[7:8, 0:1]
        high, mid, low = [p.astype(F32) for p in split3(GEOMETRY_WEIGHT * g_1)]
        yf[0:1, at] = high
        yf[1:2, at] = mid
        yf[2:3, at] = low
        high, mid, low = [p.astype(F32) for p in split3(GEOMETRY_WEIGHT * g_0)]
        for spot, piece in zip(range(3, 9), (high, mid, low, high, mid, high)):
            yf[spot:spot + 1, at] = piece
    rhs[512:544, :] = yf[...].astype(BF16)

    def column_fold(values):
        top = jnp.max(values, axis=0, keepdims=True)
        before = colmax[...]
        now = jnp.maximum(before, top)
        colsum[...] = colsum[...] * jnp.exp2(before - now) + jnp.sum(
            jnp.exp2(values - now), axis=0, keepdims=True
        )
        colmax[...] = now

    def column_start():
        colmax[...] = jnp.full_like(colmax, -1e30)
        colsum[...] = jnp.zeros_like(colsum)

    group = 4 * tgt_n
    rank = me % group
    level = me // group
    first_near = level * group

    def joined(parts):
        top = jnp.max(parts, axis=0)
        return top, jnp.sum(jnp.exp2(parts - top[None]), axis=0)

    def exchange(slots, slot, count, send_sem, recv_sem, peer):
        for k in range(1, count):
            pltpu.make_async_remote_copy(
                src_ref=slots.at[slot], dst_ref=slots.at[slot],
                send_sem=send_sem, recv_sem=recv_sem,
                device_id=peer(k), device_id_type=MESH,
            ).start()
        whole = slots.at[pl.ds(0, count - 1)]
        every = pltpu.make_async_remote_copy(
            src_ref=whole, dst_ref=whole, send_sem=send_sem, recv_sem=recv_sem,
            device_id=peer(1), device_id_type=MESH,
        )
        every.wait_recv()
        return every

    def share(turn):
        held = colmax[...] + jnp.log2(colsum[...])
        for c in range(lanes):
            near[turn, rank, c:c + 1, :] = held[:, c * 128:(c + 1) * 128]
        close = exchange(
            near.at[turn], rank, group, near_send.at[turn], near_recv.at[turn],
            lambda k: place(first_near + (rank + k) % group),
        )
        top, total = joined(near[turn])
        far[turn, level] = top + jnp.log2(total)
        wide_range = exchange(
            far.at[turn], level, n // group, far_send.at[turn], far_recv.at[turn],
            lambda k: place((me + k * group) % n),
        )
        top, total = joined(far[turn])
        value = jnp.log2(tmass[...].reshape(lanes, 128)) - (top + jnp.log2(total))
        for c in range(lanes):
            gpot[0:1, c * 128:(c + 1) * 128] = value[c:c + 1, :]
        return close, wide_range

    fetch_expr.wait()

    column_start()

    def scores(c, carry):
        src = pl.ds(pl.multiple_of(base + c * step, 128), step)
        e_s = right[0:128, src]
        a = jnp.concatenate([xs[:, pl.ds(pl.multiple_of(c * step, 128), step)], e_s], axis=0)
        b = jnp.concatenate([e_s, e_s], axis=0)
        tile = dot(a, rhs[0:256, :], ((0,), (0,)))
        tile = tile + dot(b, rhs[256:512, :], ((0,), (0,)))
        tile = tile + dot(right[128:160, src], rhs[512:544, :], ((0,), (0,)))
        tile = tile * KAPPA
        score[pl.ds(pl.multiple_of(c * step, 128), step), :] = tile
        column_fold(tile)
        return carry

    lax.fori_loop(0, rows // step, scores, 0, unroll=2)
    first = share(0)
    for copy, onward in list(zip(across, along))[2::3]:
        copy.wait_recv()
        onward.start()

    pick = lax.broadcasted_iota(jnp.int32, (32, 256), 0)
    side = lax.broadcasted_iota(jnp.int32, (32, 256), 1) // 128
    select = jnp.where(
        (pick >= 12 + 3 * side) & (pick < 15 + 3 * side), 1.0, 0.0
    ).astype(BF16)

    def source_columns(c):
        src = pl.ds(pl.multiple_of(base + c * step, 128), step)
        both = dot(right[128:160, src], select, ((0,), (0,)))
        return both[:, 0:1], both[:, 128:129]

    column_start()

    def middle_pass(c, carry):
        tile = score[pl.ds(pl.multiple_of(c * step, 128), step), :]
        log_mass, unused = source_columns(c)
        a = tile + gpot[...]
        top = jnp.max(a, axis=1, keepdims=True)
        total = jnp.sum(jnp.exp2(a - top), axis=1, keepdims=True)
        moved = log_mass - (top + jnp.log2(total))
        column_fold(tile + moved)
        return carry

    lax.fori_loop(0, rows // step, middle_pass, 0, unroll=2)
    second = share(1)

    for copy in along[2::3]:
        copy.wait_recv()
    gene_rows = genes[...].reshape(nt, genes.shape[2])

    def last_pass(c, carry):
        at = pl.ds(pl.multiple_of(c * step, 128), step)
        log_mass, mass = source_columns(c)
        a = score[at, :] + gpot[...]
        top = jnp.max(a, axis=1, keepdims=True)
        p = jnp.exp2(a - top)
        total = jnp.sum(p, axis=1, keepdims=True)
        potential = log_mass - (top + jnp.log2(total))
        numerator = dot(p.astype(BF16), gene_rows, ((1,), (0,)))
        out_ref[at, :] = (numerator * (jnp.exp2(potential + top) / mass)).astype(BF16)
        return carry

    lax.fori_loop(0, rows // step, last_pass, 0, unroll=2)

    for copy in across + along + masses + list(first) + list(second):
        copy.wait_send()
    for tile in range(TILES):
        @pl.when(jnp.logical_not(mine(tile)))
        def _():
            to_owner(tile).wait_send()

    @pl.when(owns)
    def _():
        whole = collected.at[pl.ds(0, n - 1)]
        pltpu.make_async_remote_copy(
            src_ref=whole, dst_ref=whole, send_sem=ag_send, recv_sem=rs_recv,
            device_id=place((me + 1) % n), device_id_type=MESH,
        ).wait_send()


def shards(src_n, tgt_n, es, et, xs, xt, plan, ms, mt, fs, genes):
    n = src_n * tgt_n
    local = es.shape[1]
    cols = et.shape[1]
    nt = cols * tgt_n
    rows = local // tgt_n
    step = min(rows, 512) if nt <= 1024 else 128
    total_pairs = float(local * src_n * nt)
    gene_count = genes.shape[1]
    body = functools.partial(kernel, src_n, tgt_n, total_pairs, rows, step)
    anywhere = pl.BlockSpec(memory_space=pl.ANY)
    vmem = pl.BlockSpec(memory_space=pltpu.VMEM)
    dma = pltpu.SemaphoreType.DMA
    return pl.pallas_call(
        body,
        out_shape=jax.ShapeDtypeStruct((rows, gene_count), BF16),
        in_specs=[anywhere, vmem, anywhere, vmem, anywhere, vmem, vmem, vmem, anywhere],
        out_specs=vmem,
        scratch_shapes=[
            pltpu.VMEM((160, local), BF16),
            pltpu.VMEM((32, local), F32),
            pltpu.VMEM((local, cols), BF16),
            pltpu.VMEM((128, rows), BF16),
            pltpu.VMEM((tgt_n, 128, cols), BF16),
            pltpu.VMEM((tgt_n, 128, cols), BF16),
            pltpu.VMEM((tgt_n, cols // 128, 128), F32),
            pltpu.VMEM((tgt_n, cols, gene_count), BF16),
            pltpu.VMEM((TILES, 8, 128), F32),
            pltpu.VMEM((n, 8, 128), F32),
            pltpu.VMEM((TILES, 8, 128), F32),
            pltpu.VMEM((544, nt), BF16),
            pltpu.VMEM((32, nt), F32),
            pltpu.VMEM((rows, nt), F32),
            pltpu.VMEM((2, 4 * tgt_n, nt // 128, 128), F32),
            pltpu.VMEM((2, src_n // 4, nt // 128, 128), F32),
            pltpu.VMEM((1, nt), F32),
            pltpu.VMEM((1, nt), F32),
            pltpu.VMEM((1, nt), F32),
            dma((3 + CHUNKS,)),
            dma((4, tgt_n - 1)),
            dma((4, tgt_n - 1)),
            dma((3, tgt_n - 1)),
            dma((3, tgt_n - 1)),
            dma((TILES,)),
            dma,
            dma,
            dma((TILES,)),
            dma((2,)),
            dma((2,)),
            dma((2,)),
            dma((2,)),
        ],
        compiler_params=pltpu.CompilerParams(
            collective_id=0, has_side_effects=True, vmem_limit_bytes=56 * 1024 * 1024
        ),
    )(
        es, et, xs, xt, plan,
        ms.reshape(1, local), mt.reshape(cols // 128, 128), fs.reshape(1, local), genes,
    )


def solution(mesh):
    src_n = mesh.shape["src"]
    tgt_n = mesh.shape["tgt"]
    return jax.shard_map(
        functools.partial(shards, src_n, tgt_n),
        mesh=mesh,
        in_specs=(
            P(None, "src"),
            P(None, "tgt"),
            P(None, "src"),
            P(None, "tgt"),
            P("src", "tgt"),
            P("src"),
            P("tgt"),
            P("src"),
            P("tgt", None),
        ),
        out_specs=P(("src", "tgt"), None),
        check_vma=False,
    )
```

```python
import functools
import math

import jax
import jax.numpy as jnp
from jax import lax
from jax.experimental import pallas as pl
from jax.experimental.pallas import tpu as pltpu
from jax.sharding import PartitionSpec as P

EPSILON = 0.05
GEOMETRY_WEIGHT = 4.0
LOG2E = math.log2(math.e)
KAPPA = 2.0 * LOG2E / EPSILON
MESH = pl.DeviceIdType.MESH
F32 = jnp.float32
BF16 = jnp.bfloat16
TILES = 17
CHUNKS = 4
HIGHEST = lax.Precision.HIGHEST


def split3(value):
    high = value.astype(BF16)
    rest = value - high.astype(F32)
    middle = rest.astype(BF16)
    low = (rest - middle.astype(F32)).astype(BF16)
    return high, middle, low


def dot(a, b, dims):
    return lax.dot_general(a, b, (dims, ((), ())), preferred_element_type=F32)


def dot3(a, b, dims):
    high, middle, low = split3(a)
    return dot(high, b, dims) + (dot(middle, b, dims) + dot(low, b, dims))


def exact(a, b, dims):
    return lax.dot_general(a, b, (dims, ((), ())), precision=HIGHEST, preferred_element_type=F32)


def kernel(
    src_n, tgt_n, total_pairs, rows, step,
    es_ref, et_ref, xs_ref, xt_ref, plan_ref, ms_ref, mt_ref, fs_ref, genes_ref,
    out_ref,
    right, xf, plan, xs, emb, expr, tmass, genes, partial, collected, core,
    rhs, yf, score, near, far, gpot, colmax, colsum,
    in_sem, tgt_send, tgt_recv, fw_send, fw_recv, rs_send, rs_recv, ag_send, ag_recv,
    near_send, near_recv, far_send, far_recv,
):
    n = src_n * tgt_n
    s = lax.axis_index("src")
    t = lax.axis_index("tgt")
    me = s * tgt_n + t
    cols = et_ref.shape[1]
    nt = cols * tgt_n
    local = es_ref.shape[1]
    lanes = nt // 128
    base = t * rows

    def place(linear):
        return (linear // tgt_n, linear % tgt_n)

    def owner(tile):
        return (tile, tile % 2) if tile < 16 else (0, 1)

    barrier = pltpu.get_barrier_semaphore()

    def greet(k, carry):
        pl.semaphore_signal(barrier, inc=1, device_id=place((me + k) % n), device_id_type=MESH)
        return carry

    lax.fori_loop(1, n, greet, 0)

    plan_step = local // CHUNKS
    fetch_embed = pltpu.make_async_copy(es_ref, right.at[0:128], in_sem.at[0])
    fetch_plan = [
        pltpu.make_async_copy(
            plan_ref.at[c * plan_step:(c + 1) * plan_step],
            plan.at[c * plan_step:(c + 1) * plan_step], in_sem.at[3 + c],
        )
        for c in range(CHUNKS)
    ]
    fetch_expr = pltpu.make_async_copy(
        xs_ref.at[:, pl.ds(pl.multiple_of(base, 128), rows)], xs, in_sem.at[1]
    )
    fetch_genes = pltpu.make_async_copy(genes_ref, genes.at[t], in_sem.at[2])
    for copy in [fetch_embed] + fetch_plan + [fetch_expr, fetch_genes]:
        copy.start()
    fetch_embed.wait()

    wide = right[0:128, :].astype(F32)
    q_src = jnp.sum(wide * wide, axis=0, keepdims=True)
    xf[...] = jnp.zeros_like(xf)
    xf[0:3, :] = jnp.ones((3, local), F32)

    def put(ref, value, spots):
        pieces = split3(value)
        for piece, places in zip(pieces, spots):
            for at in places:
                ref[at:at + 1, :] = piece.astype(F32)

    put(xf, q_src, ((3, 4, 5), (6, 7), (8,)))
    put(xf, 0.5 * fs_ref[...], ((9,), (10,), (11,)))
    put(xf, jnp.log2(ms_ref[...]), ((12,), (13,), (14,)))
    put(xf, ms_ref[...], ((15,), (16,), (17,)))
    right[128:160, :] = xf[...].astype(BF16)

    pl.semaphore_wait(barrier, n - 1)

    half = s % 2
    sibling = (s + 1 - 2 * half, t)

    def part(size):
        return pl.ds(pl.multiple_of(half * (size // 2), size // 2), size // 2)

    emb_part, gene_part = part(128), part(cols)
    across, along = [], []
    for d in range(1, tgt_n):
        peer = (s, (t + d) % tgt_n)
        other = (t + tgt_n - d) % tgt_n
        for a, (ref, held, piece) in enumerate(
            ((et_ref, emb, emb_part), (xt_ref, expr, emb_part), (genes.at[t], genes, gene_part))
        ):
            across.append(
                pltpu.make_async_remote_copy(
                    src_ref=ref.at[piece], dst_ref=held.at[t, piece],
                    send_sem=tgt_send.at[a, d - 1], recv_sem=tgt_recv.at[a, d - 1],
                    device_id=peer, device_id_type=MESH,
                )
            )
            along.append(
                pltpu.make_async_remote_copy(
                    src_ref=held.at[other, piece], dst_ref=held.at[other, piece],
                    send_sem=fw_send.at[a, d - 1], recv_sem=fw_recv.at[a, d - 1],
                    device_id=sibling, device_id_type=MESH,
                )
            )
    masses = [
        pltpu.make_async_remote_copy(
            src_ref=mt_ref, dst_ref=tmass.at[t],
            send_sem=tgt_send.at[3, d - 1], recv_sem=tgt_recv.at[3, d - 1],
            device_id=(s, (t + d) % tgt_n), device_id_type=MESH,
        )
        for d in range(1, tgt_n)
    ]
    for copy in across[0::3] + across[1::3] + masses:
        copy.start()
    emb[t] = et_ref[...]
    expr[t] = xt_ref[...]
    tmass[t] = mt_ref[...]

    here = 0.0
    for c in range(CHUNKS):
        fetch_plan[c].wait()
        at = slice(c * plan_step, (c + 1) * plan_step)
        here = here + dot(right[:, at], plan[at, :], ((1,), (0,)))
    target = et_ref[...]
    target_wide = target.astype(F32)
    q_tgt = jnp.sum(target_wide * target_wide, axis=0, keepdims=True)
    by_e = here[0:128, :]
    by_one = here[128:129, :]
    by_q = here[131:132, :] + (here[134:135, :] + here[136:137, :])
    partial[0:16] = dot3(by_e, target, ((1,), (1,))).reshape(16, 8, 128)
    row = lax.broadcasted_iota(jnp.int32, (8, cols), 0)
    pair = jnp.where(row == 0, 1.0, jnp.where(row == 1, q_tgt, 0.0))
    sums = jnp.where(row == 2, by_one, jnp.where(row == 3, by_q, 0.0))
    border = exact(pair, by_e, ((1,), (1,))) + dot3(sums, target, ((1,), (1,)))
    scalar_rows = jnp.where(
        row == 4, by_one,
        jnp.where(row == 5, by_one * q_tgt, jnp.where(row == 6, by_q, jnp.where(row == 7, by_q * q_tgt, 0.0))),
    )
    border = border + jnp.sum(scalar_rows, axis=1, keepdims=True)
    partial[16] = border

    def to_owner(tile):
        return pltpu.make_async_remote_copy(
            src_ref=partial.at[tile], dst_ref=collected.at[me],
            send_sem=rs_send.at[tile], recv_sem=rs_recv,
            device_id=owner(tile), device_id_type=MESH,
        )

    def mine(tile):
        return (s == owner(tile)[0]) & (t == owner(tile)[1])

    for tile in range(TILES):
        @pl.when(jnp.logical_not(mine(tile)))
        def _():
            to_owner(tile).start()

    for copy, onward in list(zip(across, along))[0::3] + list(zip(across, along))[1::3]:
        copy.wait_recv()
        onward.start()

    own_tile = jnp.where((s == 0) & (t == 1), 16, jnp.minimum(s, 15))
    owns = ((s < 16) & (t == s % 2)) | ((s == 0) & (t == 1))

    @pl.when(owns)
    def _():
        collected[me] = partial[own_tile]
        whole = collected.at[pl.ds(0, n - 1)]
        pltpu.make_async_remote_copy(
            src_ref=whole, dst_ref=whole, send_sem=ag_send, recv_sem=rs_recv,
            device_id=place((me + 1) % n), device_id_type=MESH,
        ).wait_recv()
        core[own_tile] = jnp.sum(collected[...], axis=0)

        def spread(k, carry):
            pltpu.make_async_remote_copy(
                src_ref=core.at[own_tile], dst_ref=core.at[own_tile],
                send_sem=ag_send, recv_sem=ag_recv.at[own_tile],
                device_id=place((me + k) % n), device_id_type=MESH,
            ).start()
            return carry

        lax.fori_loop(1, n, spread, 0)

    for copy in along[0::3] + along[1::3] + masses:
        copy.wait_recv()

    for tile in range(TILES):
        @pl.when(jnp.logical_not(mine(tile)))
        def _():
            pltpu.make_async_remote_copy(
                src_ref=core.at[tile], dst_ref=core.at[tile],
                send_sem=ag_send, recv_sem=ag_recv.at[tile],
                device_id=place((me + 1) % n), device_id_type=MESH,
            ).wait_recv()

    fetch_genes.wait()
    for copy in across[2::3]:
        copy.start()

    middle = core[0:16].reshape(128, 128) / total_pairs
    edge = core[16] / total_pairs
    yf[...] = jnp.zeros_like(yf)
    yf[9:12, :] = jnp.ones((3, nt), F32)
    row8 = lax.broadcasted_iota(jnp.int32, (8, cols), 0)
    for block in range(tgt_n):
        at = slice(block * cols, (block + 1) * cols)
        e_t = emb[block]
        e_wide = e_t.astype(F32)
        q_t = jnp.sum(e_wide * e_wide, axis=0, keepdims=True)
        ends = jnp.where(row8 == 0, q_t, jnp.where(row8 == 1, 1.0, 0.0))
        g_e = -2.0 * dot3(middle, e_t, ((1,), (0,))) + exact(edge, ends, ((0,), (0,)))
        high, mid, low = split3((-2.0 * GEOMETRY_WEIGHT) * g_e)
        rhs[0:128, at] = expr[block]
        rhs[128:256, at] = high
        rhs[256:384, at] = mid
        rhs[384:512, at] = low
        g_x = -2.0 * dot3(edge, e_t, ((1,), (0,)))
        g_0 = g_x[2:3, :] + edge[4:5, 0:1] * q_t + edge[5:6, 0:1]
        g_1 = g_x[3:4, :] + edge[6:7, 0:1] * q_t + edge[7:8, 0:1]
        high, mid, low = [p.astype(F32) for p in split3(GEOMETRY_WEIGHT * g_1)]
        yf[0:1, at] = high
        yf[1:2, at] = mid
        yf[2:3, at] = low
        high, mid, low = [p.astype(F32) for p in split3(GEOMETRY_WEIGHT * g_0)]
        for spot, piece in zip(range(3, 9), (high, mid, low, high, mid, high)):
            yf[spot:spot + 1, at] = piece
    rhs[512:544, :] = yf[...].astype(BF16)

    def column_fold(values):
        top = jnp.max(values, axis=0, keepdims=True)
        before = colmax[...]
        now = jnp.maximum(before, top)
        colsum[...] = colsum[...] * jnp.exp2(before - now) + jnp.sum(
            jnp.exp2(values - now), axis=0, keepdims=True
        )
        colmax[...] = now

    def column_start():
        colmax[...] = jnp.full_like(colmax, -1e30)
        colsum[...] = jnp.zeros_like(colsum)

    group = 4 * tgt_n
    rank = me % group
    level = me // group
    first_near = level * group

    def joined(parts):
        top = jnp.max(parts, axis=0)
        return top, jnp.sum(jnp.exp2(parts - top[None]), axis=0)

    def exchange(slots, slot, count, send_sem, recv_sem, peer):
        for k in range(1, count):
            pltpu.make_async_remote_copy(
                src_ref=slots.at[slot], dst_ref=slots.at[slot],
                send_sem=send_sem, recv_sem=recv_sem,
                device_id=peer(k), device_id_type=MESH,
            ).start()
        whole = slots.at[pl.ds(0, count - 1)]
        every = pltpu.make_async_remote_copy(
            src_ref=whole, dst_ref=whole, send_sem=send_sem, recv_sem=recv_sem,
            device_id=peer(1), device_id_type=MESH,
        )
        every.wait_recv()
        return every

    def share(turn):
        held = colmax[...] + jnp.log2(colsum[...])
        for c in range(lanes):
            near[turn, rank, c:c + 1, :] = held[:, c * 128:(c + 1) * 128]
        close = exchange(
            near.at[turn], rank, group, near_send.at[turn], near_recv.at[turn],
            lambda k: place(first_near + (rank + k) % group),
        )
        top, total = joined(near[turn])
        far[turn, level] = top + jnp.log2(total)
        wide_range = exchange(
            far.at[turn], level, n // group, far_send.at[turn], far_recv.at[turn],
            lambda k: place((me + k * group) % n),
        )
        top, total = joined(far[turn])
        value = jnp.log2(tmass[...].reshape(lanes, 128)) - (top + jnp.log2(total))
        for c in range(lanes):
            gpot[0:1, c * 128:(c + 1) * 128] = value[c:c + 1, :]
        return close, wide_range

    fetch_expr.wait()

    column_start()

    def scores(c, carry):
        src = pl.ds(pl.multiple_of(base + c * step, 128), step)
        e_s = right[0:128, src]
        a = jnp.concatenate([xs[:, pl.ds(pl.multiple_of(c * step, 128), step)], e_s], axis=0)
        b = jnp.concatenate([e_s, e_s], axis=0)
        tile = dot(a, rhs[0:256, :], ((0,), (0,)))
        tile = tile + dot(b, rhs[256:512, :], ((0,), (0,)))
        tile = tile + dot(right[128:160, src], rhs[512:544, :], ((0,), (0,)))
        tile = tile * KAPPA
        score[pl.ds(pl.multiple_of(c * step, 128), step), :] = tile
        column_fold(tile)
        return carry

    lax.fori_loop(0, rows // step, scores, 0, unroll=4)
    first = share(0)
    for copy, onward in list(zip(across, along))[2::3]:
        copy.wait_recv()
        onward.start()

    pick = lax.broadcasted_iota(jnp.int32, (32, 256), 0)
    side = lax.broadcasted_iota(jnp.int32, (32, 256), 1) // 128
    select = jnp.where(
        (pick >= 12 + 3 * side) & (pick < 15 + 3 * side), 1.0, 0.0
    ).astype(BF16)

    def source_columns(c):
        src = pl.ds(pl.multiple_of(base + c * step, 128), step)
        both = dot(right[128:160, src], select, ((0,), (0,)))
        return both[:, 0:1], both[:, 128:129]

    column_start()

    def middle_pass(c, carry):
        tile = score[pl.ds(pl.multiple_of(c * step, 128), step), :]
        log_mass, unused = source_columns(c)
        a = tile + gpot[...]
        top = jnp.max(a, axis=1, keepdims=True)
        total = jnp.sum(jnp.exp2(a - top), axis=1, keepdims=True)
        moved = log_mass - (top + jnp.log2(total))
        column_fold(tile + moved)
        return carry

    lax.fori_loop(0, rows // step, middle_pass, 0, unroll=4)
    second = share(1)

    for copy in along[2::3]:
        copy.wait_recv()
    gene_rows = genes[...].reshape(nt, genes.shape[2])

    def last_pass(c, carry):
        at = pl.ds(pl.multiple_of(c * step, 128), step)
        log_mass, mass = source_columns(c)
        a = score[at, :] + gpot[...]
        top = jnp.max(a, axis=1, keepdims=True)
        p = jnp.exp2(a - top)
        total = jnp.sum(p, axis=1, keepdims=True)
        potential = log_mass - (top + jnp.log2(total))
        numerator = dot(p.astype(BF16), gene_rows, ((1,), (0,)))
        out_ref[at, :] = (numerator * (jnp.exp2(potential + top) / mass)).astype(BF16)
        return carry

    lax.fori_loop(0, rows // step, last_pass, 0, unroll=4)

    for copy in across + along + masses + list(first) + list(second):
        copy.wait_send()
    for tile in range(TILES):
        @pl.when(jnp.logical_not(mine(tile)))
        def _():
            to_owner(tile).wait_send()

    @pl.when(owns)
    def _():
        whole = collected.at[pl.ds(0, n - 1)]
        pltpu.make_async_remote_copy(
            src_ref=whole, dst_ref=whole, send_sem=ag_send, recv_sem=rs_recv,
            device_id=place((me + 1) % n), device_id_type=MESH,
        ).wait_send()


def shards(src_n, tgt_n, es, et, xs, xt, plan, ms, mt, fs, genes):
    n = src_n * tgt_n
    local = es.shape[1]
    cols = et.shape[1]
    nt = cols * tgt_n
    rows = local // tgt_n
    step = min(rows, 512) if nt <= 1024 else 128
    total_pairs = float(local * src_n * nt)
    gene_count = genes.shape[1]
    body = functools.partial(kernel, src_n, tgt_n, total_pairs, rows, step)
    anywhere = pl.BlockSpec(memory_space=pl.ANY)
    vmem = pl.BlockSpec(memory_space=pltpu.VMEM)
    dma = pltpu.SemaphoreType.DMA
    return pl.pallas_call(
        body,
        out_shape=jax.ShapeDtypeStruct((rows, gene_count), BF16),
        in_specs=[anywhere, vmem, anywhere, vmem, anywhere, vmem, vmem, vmem, anywhere],
        out_specs=vmem,
        scratch_shapes=[
            pltpu.VMEM((160, local), BF16),
            pltpu.VMEM((32, local), F32),
            pltpu.VMEM((local, cols), BF16),
            pltpu.VMEM((128, rows), BF16),
            pltpu.VMEM((tgt_n, 128, cols), BF16),
            pltpu.VMEM((tgt_n, 128, cols), BF16),
            pltpu.VMEM((tgt_n, cols // 128, 128), F32),
            pltpu.VMEM((tgt_n, cols, gene_count), BF16),
            pltpu.VMEM((TILES, 8, 128), F32),
            pltpu.VMEM((n, 8, 128), F32),
            pltpu.VMEM((TILES, 8, 128), F32),
            pltpu.VMEM((544, nt), BF16),
            pltpu.VMEM((32, nt), F32),
            pltpu.VMEM((rows, nt), F32),
            pltpu.VMEM((2, 4 * tgt_n, nt // 128, 128), F32),
            pltpu.VMEM((2, src_n // 4, nt // 128, 128), F32),
            pltpu.VMEM((1, nt), F32),
            pltpu.VMEM((1, nt), F32),
            pltpu.VMEM((1, nt), F32),
            dma((3 + CHUNKS,)),
            dma((4, tgt_n - 1)),
            dma((4, tgt_n - 1)),
            dma((3, tgt_n - 1)),
            dma((3, tgt_n - 1)),
            dma((TILES,)),
            dma,
            dma,
            dma((TILES,)),
            dma((2,)),
            dma((2,)),
            dma((2,)),
            dma((2,)),
        ],
        compiler_params=pltpu.CompilerParams(
            collective_id=0, has_side_effects=True, vmem_limit_bytes=56 * 1024 * 1024
        ),
    )(
        es, et, xs, xt, plan,
        ms.reshape(1, local), mt.reshape(cols // 128, 128), fs.reshape(1, local), genes,
    )


def solution(mesh):
    src_n = mesh.shape["src"]
    tgt_n = mesh.shape["tgt"]
    return jax.shard_map(
        functools.partial(shards, src_n, tgt_n),
        mesh=mesh,
        in_specs=(
            P(None, "src"),
            P(None, "tgt"),
            P(None, "src"),
            P(None, "tgt"),
            P("src", "tgt"),
            P("src"),
            P("tgt"),
            P("src"),
            P("tgt", None),
        ),
        out_specs=P(("src", "tgt"), None),
        check_vma=False,
    )
```
